32 devices in a mesh: ic: 4 (over z_hi, core), member: 2 (over z_lo), lat: 4 (over y, x).
Axes of the slice: x: 2, y: 2, z: 4 (z_hi: 2, z_lo: 2; z = z_hi * 2 + z_lo), core: 2. Of those that a mesh axis runs over, the one named last changes fastest.
Arguments:
- state: bfloat16 [8, 640, 32, 2560], P(('ic', 'member'), 'lat'), parts along dimension 0, may hold values from -6 to 6
- target: bfloat16 [2560, 32, 2560], P(('ic', 'lat')), parts along dimension 0, may hold values from -6 to 6
- noise: float32 [8, 640, 32, 320], P(('ic', 'member'), 'lat'), parts along dimension 0, may hold values from -4 to 4
- gain: float32 [640, 320], P('lat'), may hold values from 0.2 to 1
- vertical_mix: float32 [32, 32], replicated, may hold values from -1 to 1
Outputs:
- new_state: bfloat16 [8, 640, 32, 2560], P(('ic', 'member'), 'lat'), parts along dimension 0
- crps: float32 [8, 640, 2560], P(('ic', 'member'), 'lat'), parts along dimension 0
The draws below stay inside these ranges and needn't reach their ends.
There are 4 independent parts, one for each index of `ic`. The reference program is written for one: setup_inputs(seed, part) draws one part's arguments, and reference() takes and returns one part's arrays. A program takes and returns all parts, laid end to end along the dimension named above; an argument that names none is the same for every part. Nothing has to cross between parts.
All inputs are finite; a program needn't handle non-finite values.
Results may differ from the reference program's by a relative error of at most 0.0042.
Values may be sent and summed in bfloat16 or wider, within the bound.
A program may use at most 256 MiB of HBM per device.

```python
import math
import jax
import jax.numpy as jnp
from jax import lax

NLON = 2560
NLAT = 640
MW = 320
LEVELS = 32
MEMBERS = 2
NK = 320


def shard_levels(key, shape, pieces, low, top_value):
    level = 1.0
    for dim, parts in pieces:
        draws = jax.random.uniform(jax.random.fold_in(jax.random.fold_in(key, 6), dim), (parts,), jnp.float32, low / len(pieces), top_value / len(pieces))
        level = level * jnp.repeat(jnp.exp(draws), shape[dim] // parts).reshape((-1,) + (1,) * (len(shape) - 1 - dim))
    return level


def centred(key, dims, width, bound, shards=(), held_as=jnp.bfloat16):
    result = width * jax.random.normal(key, dims, jnp.float32)
    if shards:
        result = result * shard_levels(key, dims, shards, -0.22, 0.18)
    return jnp.clip(result, -bound, bound).astype(held_as)


def setup_inputs(seed: int = 0, part: int = 0) -> dict:
    seeds = jax.random.split(jax.random.key(seed), 6)
    part_keys = jax.random.split(jax.random.fold_in(seeds[5], part), 6)
    return {
        "state": centred(part_keys[0], (MEMBERS, NLAT, LEVELS, NLON), 1.0, 6.0, ((0, 2), (1, 4))),
        "target": centred(part_keys[1], (NLAT, LEVELS, NLON), 1.0, 6.0, ((0, 4),)),
        "noise": centred(part_keys[2], (MEMBERS, 2 * MW, LEVELS, NK), 0.5, 4.0, ((0, 2), (1, 4)), jnp.float32),
        "gain": jnp.clip(jnp.exp(math.log(1.0) - 1.609438 * jax.random.uniform(seeds[3], (2 * MW, NK), jnp.float32) ** shard_levels(seeds[3], (2 * MW, NK), ((0, 4),), -0.2, 0.2)), 0.2, 1.0),
        "vertical_mix": centred(seeds[4], (LEVELS, LEVELS), LEVELS ** -0.5, 1.0, (), jnp.float32),
    }


def column_info():
    column = jnp.arange(2 * MW, dtype=jnp.int32)
    part = column // MW
    rest = column % MW
    half = MW // 2
    wave = jnp.where(rest < half, 2 * rest + 2 * part, 2 * (rest - half) + 1)
    return (part, wave, rest >= half)

def lon_table():
    part, wave, odd = column_info()
    place = jnp.arange(NLON, dtype=jnp.int32)
    phase = place[:, None] * wave[None, :] % NLON
    angle = phase.astype(jnp.float32) * jnp.float32(2.0 * math.pi / NLON)
    return jnp.where(part[None, :] == 0, jnp.cos(angle), jnp.sin(angle)).astype(jnp.bfloat16)

def lat_bases():
    theta = (jnp.arange(NLAT, dtype=jnp.float32) + 0.5) * jnp.float32(math.pi / NLAT)
    modes = jnp.arange(NLAT // 2, dtype=jnp.float32)
    even = jnp.cos(modes[:, None] * theta[None, :])
    odd = jnp.sin((modes[:, None] + 1.0) * theta[None, :])
    return (even, odd)

def member_score(own, other, truth):
    own = own.astype(jnp.float32)
    other = other.astype(jnp.float32)
    truth = truth.astype(jnp.float32)
    skill = lax.optimization_barrier(jnp.mean(jnp.abs(own - truth), axis=1))
    spread = lax.optimization_barrier(jnp.mean(jnp.abs(own - other), axis=1))
    return skill - 0.5 * spread

def reference(state, target, noise, gain, vertical_mix):
    table = lon_table()
    even, odd_basis = lat_bases()
    part, wave, odd = column_info()
    modes = NLAT // 2
    levels = state.shape[2]
    highest = lax.Precision.HIGHEST
    outputs = []
    for member in range(MEMBERS):
        field = state[member]
        zonal = jnp.dot(field.reshape(NLAT * levels, NLON), table, preferred_element_type=jnp.float32)
        zonal = (zonal * jnp.float32(1.0 / math.sqrt(NLON))).reshape(NLAT, levels * 2 * MW)
        spec_even = jnp.dot(even, zonal, precision=highest).reshape(modes, levels, 2 * MW)
        spec_odd = jnp.dot(odd_basis, zonal, precision=highest).reshape(modes, levels, 2 * MW)
        spectral = jnp.where(odd[None, None, :], spec_odd, spec_even) * jnp.float32(math.sqrt(2.0 / NLAT))
        forced = gain.T[:, None, :] * spectral + jnp.transpose(noise[member], (2, 1, 0))
        flat = forced.reshape(modes, levels * 2 * MW)
        back_even = jnp.dot(even.T, flat, precision=highest).reshape(NLAT, levels, 2 * MW)
        back_odd = jnp.dot(odd_basis.T, flat, precision=highest).reshape(NLAT, levels, 2 * MW)
        back = jnp.where(odd[None, None, :], back_odd, back_even) * jnp.float32(math.sqrt(2.0 / modes))
        back = back.astype(jnp.bfloat16)
        tendency = lax.dot_general(back.reshape(NLAT * levels, 2 * MW), table, (((1,), (1,)), ((), ())), preferred_element_type=jnp.float32)
        tendency = (tendency * jnp.float32(1.0 / math.sqrt(MW))).reshape(NLAT, levels, NLON)
        mixed = jnp.einsum('ab,jbi->jai', vertical_mix, tendency, precision=highest)
        outputs.append((field.astype(jnp.float32) + mixed).astype(jnp.bfloat16))
    new_state = jnp.stack(outputs, axis=0)
    crps = jnp.stack([member_score(new_state[0], new_state[1], target), member_score(new_state[1], new_state[0], target)], axis=0)
    return (new_state, crps)
```

```python
import math

import jax
import jax.numpy as jnp
from jax import lax
from jax.sharding import PartitionSpec as P


def swapped(value):
    return lax.ppermute(value, "member", [(0, 1), (1, 0)])


def column_info(mw):
    column = jnp.arange(2 * mw, dtype=jnp.int32)
    part = column // mw
    rest = column % mw
    half = mw // 2
    return part, jnp.where(rest < half, 2 * rest + 2 * part, 2 * (rest - half) + 1)


def lon_table(nlon, mw):
    part, wave = column_info(mw)
    inner = math.gcd(nlon, 64)
    outer = nlon // inner

    def angles(step, count):
        phase = (step * jnp.arange(count, dtype=jnp.int32))[:, None] * wave[None, :] % nlon
        angle = phase.astype(jnp.float32) * jnp.float32(2.0 * math.pi / nlon)
        return jnp.cos(angle), jnp.sin(angle)

    ca, sa = angles(inner, outer)
    cb, sb = angles(1, inner)
    sine = part[None, :] != 0
    first = jnp.where(sine, sa, ca)
    second = jnp.where(sine, ca, -sa)
    first, second, cb, sb = lax.optimization_barrier((first, second, cb, sb))
    table = first[:, None, :] * cb[None] + second[:, None, :] * sb[None]
    return lax.optimization_barrier(table.reshape(nlon, 2 * mw).astype(jnp.bfloat16))


def lat_basis(nlat, modes, is_odd):
    theta = (jnp.arange(nlat, dtype=jnp.float32) + 0.5) * jnp.float32(math.pi / nlat)
    k = jnp.arange(modes, dtype=jnp.float32)
    shift = jnp.where(is_odd, jnp.float32(1.0), jnp.float32(0.0))
    angle = (k[:, None] + shift) * theta[None, :]
    basis = jnp.where(is_odd, jnp.sin(angle), jnp.cos(angle))
    return lax.optimization_barrier(basis)


def body(state, target, noise, gain, vertical_mix):
    field = state[0]
    rows, levels, nlon = field.shape
    width, modes = gain.shape
    n = lax.axis_size("lat")
    nlat = rows * n
    mw = width * n // 2
    half = rows // 2
    f32, bf16 = jnp.float32, jnp.bfloat16
    high = lax.Precision.HIGH
    me = lax.axis_index("member")
    mine, theirs = me * half, (1 - me) * half

    other_state = swapped(lax.dynamic_slice_in_dim(field, theirs, half, 0))

    table = lon_table(nlon, mw)
    zonal = jnp.dot(field.reshape(rows * levels, nlon), table, preferred_element_type=f32)
    zonal = (zonal * f32(1.0 / math.sqrt(nlon))).astype(bf16)
    zonal = zonal.reshape(rows, levels, n, width).transpose(2, 0, 3, 1)
    zonal = zonal.reshape(n, rows, width * levels)
    gathered = lax.all_to_all(zonal, "lat", 0, 0, tiled=True).reshape(nlat, width * levels)

    odd = (lax.axis_index("lat") * width) % mw >= mw // 2
    basis = lat_basis(nlat, modes, odd)
    basis_hi = basis.astype(bf16)
    basis_lo = (basis - basis_hi.astype(f32)).astype(bf16)
    spectral = jnp.dot(basis_hi, gathered, preferred_element_type=f32) + jnp.dot(
        basis_lo, gathered, preferred_element_type=f32
    )
    gains = jnp.repeat(gain.T * f32(math.sqrt(2.0 / nlat)), levels, axis=1)
    forcing = noise[0].reshape(width * levels, modes).T
    gains, forcing = lax.optimization_barrier((gains, forcing))
    forced = gains * spectral + forcing
    back = jnp.dot(basis.T, forced, precision=high) * f32(math.sqrt(2.0 / modes))
    back = back.astype(bf16).reshape(n, rows, width * levels)
    returned = lax.all_to_all(back, "lat", 0, 0, tiled=True)
    returned = returned.reshape(n, rows, width, levels).transpose(1, 3, 0, 2)
    returned = returned.reshape(rows, levels, n * width)
    mixed = jnp.einsum("ab,jbc->jac", vertical_mix * f32(1.0 / math.sqrt(mw)), returned.astype(f32), precision=high)
    mixed = lax.optimization_barrier(mixed.astype(bf16))
    other_mixed = swapped(lax.dynamic_slice_in_dim(mixed, theirs, half, 0))

    def advance(start, coefficients):
        count = start.shape[0]
        move = lax.dot_general(
            coefficients.reshape(count * levels, n * width),
            table,
            (((1,), (1,)), ((), ())),
            preferred_element_type=f32,
        )
        flat = start.reshape(count * levels, nlon).astype(f32)
        return (flat + move).astype(bf16).reshape(count, levels, nlon)

    updated = advance(field, mixed)
    skill = jnp.mean(jnp.abs(updated.astype(f32) - target.astype(f32)), axis=1)
    other = advance(other_state, other_mixed)
    own = lax.dynamic_slice_in_dim(updated, mine, half, 0)
    spread = 0.5 * jnp.mean(jnp.abs(own.astype(f32) - other.astype(f32)), axis=1)
    far = swapped(spread)
    first = jnp.where(me == 0, spread, far)
    second = jnp.where(me == 0, far, spread)
    crps = skill - jnp.concatenate([first, second], axis=0)
    return (updated[None], crps[None])


def solution(mesh):
    placed = (
        P(("ic", "member"), "lat", None, None),
        P(("ic", "lat"), None, None),
        P(("ic", "member"), "lat", None, None),
        P("lat", None),
        P(),
    )
    return jax.shard_map(
        body,
        mesh=mesh,
        in_specs=placed,
        out_specs=(P(("ic", "member"), "lat", None, None), P(("ic", "member"), "lat", None)),
        check_vma=False,
    )
```

```python
import functools
import math

import jax
import jax.numpy as jnp
from jax import lax
from jax.experimental import pallas as pl
from jax.experimental.pallas import tpu as pltpu
from jax.sharding import PartitionSpec as P


def swapped(value):
    return lax.ppermute(value, "member", [(0, 1), (1, 0)])


LANES = 128
GROUP = 8


def packs(n, width, levels, rows):
    rest = width % LANES
    return (
        width // LANES == 1
        and rest * n == LANES
        and levels % n == 0
        and levels % 16 == 0
        and (rows // 2) % GROUP == 0
    )


def column_order(n, width, packed):
    column = jnp.arange(n * width, dtype=jnp.int32)
    if not packed:
        return column
    rest = width - LANES
    tail = column - n * LANES
    head = column // LANES * width + column % LANES
    return jnp.where(tail < 0, head, tail // rest * width + LANES + tail % rest)


def regroup(levels):
    row = jnp.arange(GROUP * levels, dtype=jnp.int32)
    source = row % GROUP * levels + row // GROUP
    return (source[:, None] == row[None, :]).astype(jnp.bfloat16)


def analysis_kernel(n, levels, scale, state_ref, table_ref, order_ref, out_ref):
    rows = GROUP * levels
    flat = state_ref[...].reshape(rows, state_ref.shape[2])
    zonal = jnp.dot(flat, table_ref[...], preferred_element_type=jnp.float32)
    zonal = (zonal * jnp.float32(scale)).astype(jnp.bfloat16)
    zonal = jnp.dot(order_ref[...], zonal, preferred_element_type=jnp.float32)
    for level in range(levels):
        piece = zonal[level * GROUP : (level + 1) * GROUP]
        for d in range(n):
            out_ref[d, :, level * LANES : (level + 1) * LANES] = piece[
                :, d * LANES : (d + 1) * LANES
            ].astype(jnp.bfloat16)
    rest = LANES // n
    slot = lax.broadcasted_iota(jnp.int32, (GROUP, LANES), 1) // rest
    for g in range(levels // n):
        pieces = [
            zonal[(n * g + q) * GROUP : (n * g + q + 1) * GROUP, n * LANES :] for q in range(n)
        ]
        for d in range(n):
            total = pieces[d]
            for q in range(n):
                if q != d:
                    moved = pltpu.roll(pieces[q], (q - d) % n * rest, 1)
                    total = jnp.where(slot == q, moved, total)
            at = (levels + g) * LANES
            out_ref[d, :, at : at + LANES] = total.astype(jnp.bfloat16)


def analysis(field, table, n):
    rows, levels, nlon = field.shape
    columns = table.shape[1]
    lanes = levels * columns // n
    order = regroup(levels)
    scale = 1.0 / math.sqrt(nlon)
    return pl.pallas_call(
        functools.partial(analysis_kernel, n, levels, scale),
        grid=(rows // GROUP,),
        in_specs=[
            pl.BlockSpec((GROUP, levels, nlon), lambda i: (i, 0, 0)),
            pl.BlockSpec((nlon, columns), lambda i: (0, 0)),
            pl.BlockSpec(order.shape, lambda i: (0, 0)),
        ],
        out_specs=pl.BlockSpec((n, GROUP, lanes), lambda i: (0, i, 0)),
        out_shape=jax.ShapeDtypeStruct((n, rows, lanes), jnp.bfloat16),
        cost_estimate=pl.CostEstimate(
            flops=2 * rows * levels * nlon * columns,
            bytes_accessed=2 * (field.size + n * rows * lanes),
            transcendentals=0,
        ),
        name="analysis",
    )(field, table, order)


def mix_kernel(n, levels, packed_ref, high_ref, low_ref, out_ref, flat_ref):
    rest = LANES // n
    slot = lax.broadcasted_iota(jnp.int32, (GROUP, LANES), 1) // rest
    for level in range(levels):
        for d in range(n):
            flat_ref[level * GROUP : (level + 1) * GROUP, d * LANES : (d + 1) * LANES] = packed_ref[
                d, :, level * LANES : (level + 1) * LANES
            ].astype(jnp.float32)
    for g in range(levels // n):
        at = (levels + g) * LANES
        pieces = [packed_ref[d, :, at : at + LANES].astype(jnp.float32) for d in range(n)]
        for q in range(n):
            total = pieces[q]
            for d in range(n):
                if d != q:
                    moved = pltpu.roll(pieces[d], (d - q) % n * rest, 1)
                    total = jnp.where(slot == d, moved, total)
            row = (n * g + q) * GROUP
            flat_ref[row : row + GROUP, n * LANES :] = total
    flat = flat_ref[...].astype(jnp.bfloat16)
    mixed = jnp.dot(high_ref[...], flat, preferred_element_type=jnp.float32)
    mixed += jnp.dot(low_ref[...], flat, preferred_element_type=jnp.float32)
    out_ref[...] = mixed.astype(jnp.bfloat16).reshape(out_ref.shape)


def mix(packed, weights):
    n, rows, lanes = packed.shape
    levels = weights.shape[0]
    columns = n * lanes // levels
    size = GROUP * levels
    eye = jnp.eye(GROUP, dtype=jnp.float32)
    full = weights[None, :, :, None] * eye[:, None, None, :]
    full = full.reshape(size, size)
    high = full.astype(jnp.bfloat16)
    low = (full - high.astype(jnp.float32)).astype(jnp.bfloat16)
    return pl.pallas_call(
        functools.partial(mix_kernel, n, levels),
        grid=(rows // GROUP,),
        in_specs=[
            pl.BlockSpec((n, GROUP, lanes), lambda i: (0, i, 0)),
            pl.BlockSpec((size, size), lambda i: (0, 0)),
            pl.BlockSpec((size, size), lambda i: (0, 0)),
        ],
        out_specs=pl.BlockSpec((GROUP, levels, columns), lambda i: (i, 0, 0)),
        out_shape=jax.ShapeDtypeStruct((rows, levels, columns), jnp.bfloat16),
        scratch_shapes=[pltpu.VMEM((size, columns), jnp.float32)],
        cost_estimate=pl.CostEstimate(
            flops=4 * rows * levels * size * columns,
            bytes_accessed=4 * n * rows * lanes,
            transcendentals=0,
        ),
        name="mix",
    )(packed, high, low)


def column_info(mw, column):
    part = column // mw
    rest = column % mw
    half = mw // 2
    return part, jnp.where(rest < half, 2 * rest + 2 * part, 2 * (rest - half) + 1)


def lon_table(nlon, mw, column):
    part, wave = column_info(mw, column)
    inner = math.gcd(nlon, 64)
    outer = nlon // inner

    def angles(step, count):
        phase = (step * jnp.arange(count, dtype=jnp.int32))[:, None] * wave[None, :] % nlon
        angle = phase.astype(jnp.float32) * jnp.float32(2.0 * math.pi / nlon)
        return jnp.cos(angle), jnp.sin(angle)

    ca, sa = angles(inner, outer)
    cb, sb = angles(1, inner)
    sine = part[None, :] != 0
    first = jnp.where(sine, sa, ca)
    second = jnp.where(sine, ca, -sa)
    first, second, cb, sb = lax.optimization_barrier((first, second, cb, sb))
    table = first[:, None, :] * cb[None] + second[:, None, :] * sb[None]
    return lax.optimization_barrier(table.reshape(nlon, 2 * mw).astype(jnp.bfloat16))


def lat_basis(nlat, modes, is_odd):
    theta = (jnp.arange(nlat, dtype=jnp.float32) + 0.5) * jnp.float32(math.pi / nlat)
    k = jnp.arange(modes, dtype=jnp.float32)
    shift = jnp.where(is_odd, jnp.float32(1.0), jnp.float32(0.0))
    angle = (k[:, None] + shift) * theta[None, :]
    basis = jnp.where(is_odd, jnp.sin(angle), jnp.cos(angle))
    return lax.optimization_barrier(basis)


def body(state, target, noise, gain, vertical_mix):
    field = state[0]
    rows, levels, nlon = field.shape
    width, modes = gain.shape
    n = lax.axis_size("lat")
    nlat = rows * n
    mw = width * n // 2
    half = rows // 2
    f32, bf16 = jnp.float32, jnp.bfloat16
    high = lax.Precision.HIGH
    me = lax.axis_index("member")
    mine, theirs = me * half, (1 - me) * half

    other_state = swapped(lax.dynamic_slice_in_dim(field, theirs, half, 0))

    packed = packs(n, width, levels, rows)
    table = lon_table(nlon, mw, column_order(n, width, packed))
    if packed:
        zonal = analysis(field, table, n)
    else:
        zonal = jnp.dot(field.reshape(rows * levels, nlon), table, preferred_element_type=f32)
        zonal = (zonal * f32(1.0 / math.sqrt(nlon))).astype(bf16)
        zonal = zonal.reshape(rows, levels, n, width).transpose(2, 0, 1, 3)
        zonal = zonal.reshape(n, rows, width * levels)
    gathered = lax.all_to_all(zonal, "lat", 0, 0, tiled=True).reshape(nlat, width * levels)

    odd = (lax.axis_index("lat") * width) % mw >= mw // 2
    basis = lat_basis(nlat, modes, odd)
    basis_hi = basis.astype(bf16)
    basis_lo = (basis - basis_hi.astype(f32)).astype(bf16)
    spectral = jnp.dot(basis_hi, gathered, preferred_element_type=f32) + jnp.dot(
        basis_lo, gathered, preferred_element_type=f32
    )
    cuts = ((0, LANES), (LANES, width)) if packed else ((0, width),)
    scaled = gain.T * f32(math.sqrt(2.0 / nlat))
    gains = jnp.concatenate([jnp.tile(scaled[:, a:b], (1, levels)) for a, b in cuts], axis=1)
    forcing = jnp.concatenate(
        [noise[0, a:b].transpose(2, 1, 0).reshape(modes, levels * (b - a)) for a, b in cuts], axis=1
    )
    gains, forcing = lax.optimization_barrier((gains, forcing))
    forced = gains * spectral + forcing
    back = jnp.dot(basis.T, forced, precision=high) * f32(math.sqrt(2.0 / modes))
    back = back.astype(bf16).reshape(n, rows, width * levels)
    weights = vertical_mix * f32(1.0 / math.sqrt(mw))

    def exchange(start):
        part = lax.dynamic_slice_in_dim(back, start, half, 1)
        return lax.all_to_all(part, "lat", 0, 0, tiled=True)

    def mixing(part):
        if packed:
            return mix(part, weights)
        part = part.reshape(n, half, levels, width).transpose(1, 2, 0, 3)
        part = part.reshape(half, levels, n * width).astype(f32)
        return jnp.einsum("ab,jbc->jac", weights, part, precision=high).astype(bf16)

    far_part = exchange(theirs)
    other_part = swapped(far_part)
    near_part = exchange(mine)
    near_mixed, far_mixed = mixing(near_part), mixing(far_part)
    first = jnp.where(me == 0, near_mixed, far_mixed)
    second = jnp.where(me == 0, far_mixed, near_mixed)
    mixed = lax.optimization_barrier(jnp.concatenate([first, second], axis=0))
    other_mixed = mixing(other_part)

    def advance(start, coefficients):
        count = start.shape[0]
        move = lax.dot_general(
            coefficients.reshape(count * levels, n * width),
            table,
            (((1,), (1,)), ((), ())),
            preferred_element_type=f32,
        )
        flat = start.reshape(count * levels, nlon).astype(f32)
        return (flat + move).astype(bf16).reshape(count, levels, nlon)

    updated = advance(field, mixed)
    skill = jnp.mean(jnp.abs(updated.astype(f32) - target.astype(f32)), axis=1)
    other = advance(other_state, other_mixed)
    own = lax.dynamic_slice_in_dim(updated, mine, half, 0)
    spread = 0.5 * jnp.mean(jnp.abs(own.astype(f32) - other.astype(f32)), axis=1)
    far = swapped(spread)
    first = jnp.where(me == 0, spread, far)
    second = jnp.where(me == 0, far, spread)
    crps = skill - jnp.concatenate([first, second], axis=0)
    return (updated[None], crps[None])


def solution(mesh):
    placed = (
        P(("ic", "member"), "lat", None, None),
        P(("ic", "lat"), None, None),
        P(("ic", "member"), "lat", None, None),
        P("lat", None),
        P(),
    )
    return jax.shard_map(
        body,
        mesh=mesh,
        in_specs=placed,
        out_specs=(P(("ic", "member"), "lat", None, None), P(("ic", "member"), "lat", None)),
        check_vma=False,
    )
```

```python
import functools
import math

import jax
import jax.numpy as jnp
from jax import lax
from jax.experimental import pallas as pl
from jax.experimental.pallas import tpu as pltpu
from jax.sharding import PartitionSpec as P


def swapped(value):
    return lax.ppermute(value, "member", [(0, 1), (1, 0)])


LANES = 128
GROUP = 8


def packs(n, width, levels, rows):
    rest = width % LANES
    return (
        width // LANES == 1
        and rest * n == LANES
        and levels % n == 0
        and levels % 16 == 0
        and (rows // 2) % GROUP == 0
    )


def column_order(n, width, packed):
    column = jnp.arange(n * width, dtype=jnp.int32)
    if not packed:
        return column
    rest = width - LANES
    tail = column - n * LANES
    head = column // LANES * width + column % LANES
    return jnp.where(tail < 0, head, tail // rest * width + LANES + tail % rest)


def regroup(levels):
    row = jnp.arange(GROUP * levels, dtype=jnp.int32)
    source = row % GROUP * levels + row // GROUP
    return (source[:, None] == row[None, :]).astype(jnp.bfloat16)


def analysis_kernel(n, levels, scale, state_ref, table_ref, order_ref, out_ref):
    rows = GROUP * levels
    flat = state_ref[...].reshape(rows, state_ref.shape[2])
    zonal = jnp.dot(flat, table_ref[...], preferred_element_type=jnp.float32)
    zonal = (zonal * jnp.float32(scale)).astype(jnp.bfloat16)
    zonal = jnp.dot(order_ref[...], zonal, preferred_element_type=jnp.float32)
    for level in range(levels):
        piece = zonal[level * GROUP : (level + 1) * GROUP]
        for d in range(n):
            out_ref[d, :, level * LANES : (level + 1) * LANES] = piece[
                :, d * LANES : (d + 1) * LANES
            ].astype(jnp.bfloat16)
    rest = LANES // n
    slot = lax.broadcasted_iota(jnp.int32, (GROUP, LANES), 1) // rest
    for g in range(levels // n):
        pieces = [
            zonal[(n * g + q) * GROUP : (n * g + q + 1) * GROUP, n * LANES :] for q in range(n)
        ]
        for d in range(n):
            total = pieces[d]
            for q in range(n):
                if q != d:
                    moved = pltpu.roll(pieces[q], (q - d) % n * rest, 1)
                    total = jnp.where(slot == q, moved, total)
            at = (levels + g) * LANES
            out_ref[d, :, at : at + LANES] = total.astype(jnp.bfloat16)


def analysis(field, table, n):
    rows, levels, nlon = field.shape
    columns = table.shape[1]
    lanes = levels * columns // n
    order = regroup(levels)
    scale = 1.0 / math.sqrt(nlon)
    return pl.pallas_call(
        functools.partial(analysis_kernel, n, levels, scale),
        grid=(rows // GROUP,),
        in_specs=[
            pl.BlockSpec((GROUP, levels, nlon), lambda i: (i, 0, 0)),
            pl.BlockSpec((nlon, columns), lambda i: (0, 0)),
            pl.BlockSpec(order.shape, lambda i: (0, 0)),
        ],
        out_specs=pl.BlockSpec((n, GROUP, lanes), lambda i: (0, i, 0)),
        out_shape=jax.ShapeDtypeStruct((n, rows, lanes), jnp.bfloat16),
        cost_estimate=pl.CostEstimate(
            flops=2 * rows * levels * nlon * columns,
            bytes_accessed=2 * (field.size + n * rows * lanes),
            transcendentals=0,
        ),
        name="analysis",
    )(field, table, order)


def mix_kernel(n, levels, packed_ref, high_ref, low_ref, out_ref, flat_ref):
    rest = LANES // n
    slot = lax.broadcasted_iota(jnp.int32, (GROUP, LANES), 1) // rest
    for level in range(levels):
        for d in range(n):
            flat_ref[level * GROUP : (level + 1) * GROUP, d * LANES : (d + 1) * LANES] = packed_ref[
                d, :, level * LANES : (level + 1) * LANES
            ].astype(jnp.float32)
    for g in range(levels // n):
        at = (levels + g) * LANES
        pieces = [packed_ref[d, :, at : at + LANES].astype(jnp.float32) for d in range(n)]
        for q in range(n):
            total = pieces[q]
            for d in range(n):
                if d != q:
                    moved = pltpu.roll(pieces[d], (d - q) % n * rest, 1)
                    total = jnp.where(slot == d, moved, total)
            row = (n * g + q) * GROUP
            flat_ref[row : row + GROUP, n * LANES :] = total
    flat = flat_ref[...].astype(jnp.bfloat16)
    mixed = jnp.dot(high_ref[...], flat, preferred_element_type=jnp.float32)
    mixed += jnp.dot(low_ref[...], flat, preferred_element_type=jnp.float32)
    out_ref[...] = mixed.astype(jnp.bfloat16).reshape(out_ref.shape)


def mix(packed, weights):
    n, rows, lanes = packed.shape
    levels = weights.shape[0]
    columns = n * lanes // levels
    size = GROUP * levels
    eye = jnp.eye(GROUP, dtype=jnp.float32)
    full = weights[None, :, :, None] * eye[:, None, None, :]
    full = full.reshape(size, size)
    high = full.astype(jnp.bfloat16)
    low = (full - high.astype(jnp.float32)).astype(jnp.bfloat16)
    return pl.pallas_call(
        functools.partial(mix_kernel, n, levels),
        grid=(rows // GROUP,),
        in_specs=[
            pl.BlockSpec((n, GROUP, lanes), lambda i: (0, i, 0)),
            pl.BlockSpec((size, size), lambda i: (0, 0)),
            pl.BlockSpec((size, size), lambda i: (0, 0)),
        ],
        out_specs=pl.BlockSpec((GROUP, levels, columns), lambda i: (i, 0, 0)),
        out_shape=jax.ShapeDtypeStruct((rows, levels, columns), jnp.bfloat16),
        scratch_shapes=[pltpu.VMEM((size, columns), jnp.float32)],
        cost_estimate=pl.CostEstimate(
            flops=4 * rows * levels * size * columns,
            bytes_accessed=4 * n * rows * lanes,
            transcendentals=0,
        ),
        name="mix",
    )(packed, high, low)


def column_info(mw, column):
    part = column // mw
    rest = column % mw
    half = mw // 2
    return part, jnp.where(rest < half, 2 * rest + 2 * part, 2 * (rest - half) + 1)


def lon_table(nlon, mw, column):
    part, wave = column_info(mw, column)
    inner = math.gcd(nlon, 64)
    outer = nlon // inner

    def angles(step, count):
        phase = (step * jnp.arange(count, dtype=jnp.int32))[:, None] * wave[None, :] % nlon
        angle = phase.astype(jnp.float32) * jnp.float32(2.0 * math.pi / nlon)
        return jnp.cos(angle), jnp.sin(angle)

    ca, sa = angles(inner, outer)
    cb, sb = angles(1, inner)
    sine = part[None, :] != 0
    first = jnp.where(sine, sa, ca)
    second = jnp.where(sine, ca, -sa)
    first, second, cb, sb = lax.optimization_barrier((first, second, cb, sb))
    table = first[:, None, :] * cb[None] + second[:, None, :] * sb[None]
    return lax.optimization_barrier(table.reshape(nlon, 2 * mw).astype(jnp.bfloat16))


def lat_basis(nlat, modes, is_odd):
    theta = (jnp.arange(nlat, dtype=jnp.float32) + 0.5) * jnp.float32(math.pi / nlat)
    k = jnp.arange(modes, dtype=jnp.float32)
    shift = jnp.where(is_odd, jnp.float32(1.0), jnp.float32(0.0))
    angle = (k[:, None] + shift) * theta[None, :]
    basis = jnp.where(is_odd, jnp.sin(angle), jnp.cos(angle))
    return lax.optimization_barrier(basis)


def body(state, target, noise, gain, vertical_mix):
    field = state[0]
    rows, levels, nlon = field.shape
    width, modes = gain.shape
    n = lax.axis_size("lat")
    nlat = rows * n
    mw = width * n // 2
    half = rows // 2
    f32, bf16 = jnp.float32, jnp.bfloat16
    high = lax.Precision.HIGH
    me = lax.axis_index("member")
    mine, theirs = me * half, (1 - me) * half

    quarter = half // 4
    cut = 3 * quarter

    def send(start, count):
        return swapped(lax.dynamic_slice_in_dim(field, theirs + start, count, 0))

    head_a = send(0, quarter)
    head_b = send(quarter, cut - quarter)
    tail = send(cut, half - cut)

    packed = packs(n, width, levels, rows)
    table = lon_table(nlon, mw, column_order(n, width, packed))
    if packed:
        zonal = analysis(field, table, n)
    else:
        zonal = jnp.dot(field.reshape(rows * levels, nlon), table, preferred_element_type=f32)
        zonal = (zonal * f32(1.0 / math.sqrt(nlon))).astype(bf16)
        zonal = zonal.reshape(rows, levels, n, width).transpose(2, 0, 1, 3)
        zonal = zonal.reshape(n, rows, width * levels)
    gathered = lax.all_to_all(zonal, "lat", 0, 0, tiled=True).reshape(nlat, width * levels)

    odd = (lax.axis_index("lat") * width) % mw >= mw // 2
    basis = lat_basis(nlat, modes, odd)
    basis_hi = basis.astype(bf16)
    basis_lo = (basis - basis_hi.astype(f32)).astype(bf16)
    spectral = jnp.dot(basis_hi, gathered, preferred_element_type=f32) + jnp.dot(
        basis_lo, gathered, preferred_element_type=f32
    )
    cuts = ((0, LANES), (LANES, width)) if packed else ((0, width),)
    scaled = gain.T * f32(math.sqrt(2.0 / nlat))
    gains = jnp.concatenate([jnp.tile(scaled[:, a:b], (1, levels)) for a, b in cuts], axis=1)
    forcing = jnp.concatenate(
        [noise[0, a:b].transpose(2, 1, 0).reshape(modes, levels * (b - a)) for a, b in cuts], axis=1
    )
    gains, forcing = lax.optimization_barrier((gains, forcing))
    forced = gains * spectral + forcing
    back = jnp.dot(basis.T, forced, precision=high) * f32(math.sqrt(2.0 / modes))
    back = back.astype(bf16).reshape(n, rows, width * levels)
    weights = vertical_mix * f32(1.0 / math.sqrt(mw))

    def exchange(start):
        part = lax.dynamic_slice_in_dim(back, start, half, 1)
        return lax.all_to_all(part, "lat", 0, 0, tiled=True)

    def mixing(part):
        if packed:
            return mix(part, weights)
        part = part.reshape(n, half, levels, width).transpose(1, 2, 0, 3)
        part = part.reshape(half, levels, n * width).astype(f32)
        return jnp.einsum("ab,jbc->jac", weights, part, precision=high).astype(bf16)

    far_part = exchange(theirs)
    other_part = swapped(far_part)
    near_part = exchange(mine)
    near_mixed, far_mixed = mixing(near_part), mixing(far_part)
    first = jnp.where(me == 0, near_mixed, far_mixed)
    second = jnp.where(me == 0, far_mixed, near_mixed)
    mixed = lax.optimization_barrier(jnp.concatenate([first, second], axis=0))
    other_mixed = mixing(other_part)

    def advance(start, coefficients):
        count = start.shape[0]
        move = lax.dot_general(
            coefficients.reshape(count * levels, n * width),
            table,
            (((1,), (1,)), ((), ())),
            preferred_element_type=f32,
        )
        flat = start.reshape(count * levels, nlon).astype(f32)
        return (flat + move).astype(bf16).reshape(count, levels, nlon)

    updated = advance(field, mixed)
    skill = jnp.mean(jnp.abs(updated.astype(f32) - target.astype(f32)), axis=1)
    skill = lax.optimization_barrier(skill)

    def spread_of(other_rows, start):
        count = other_rows.shape[0]
        other = advance(other_rows, lax.slice_in_dim(other_mixed, start, start + count, axis=0))
        own = lax.dynamic_slice_in_dim(updated, mine + start, count, 0)
        return 0.5 * jnp.mean(jnp.abs(own.astype(f32) - other.astype(f32)), axis=1)

    head = jnp.concatenate([spread_of(head_a, 0), spread_of(head_b, quarter)], axis=0)
    head, tail = lax.optimization_barrier((head, tail))
    last = spread_of(tail, cut)
    far = jnp.concatenate([swapped(head), swapped(last)], axis=0)
    spread = jnp.concatenate([head, last], axis=0)
    first = jnp.where(me == 0, spread, far)
    second = jnp.where(me == 0, far, spread)
    crps = skill - jnp.concatenate([first, second], axis=0)
    return (updated[None], crps[None])


def solution(mesh):
    placed = (
        P(("ic", "member"), "lat", None, None),
        P(("ic", "lat"), None, None),
        P(("ic", "member"), "lat", None, None),
        P("lat", None),
        P(),
    )
    return jax.shard_map(
        body,
        mesh=mesh,
        in_specs=placed,
        out_specs=(P(("ic", "member"), "lat", None, None), P(("ic", "member"), "lat", None)),
        check_vma=False,
    )
```
